128 devices in a mesh: rows: 16 (over y, z), cols: 8 (over x, core).
Axes of the slice: x: 4, y: 4, z: 4, core: 2. Of those that a mesh axis runs over, the one named last changes fastest.
Arguments:
- queries: bfloat16 [32768, 768], P('rows')
- candidates: bfloat16 [262144, 768], P(('rows', 'cols'))
- requests: int32 [2048, 1], P(('rows', 'cols')), may hold values from 0 to 7, as said below
- pairs: int32 [16384, 2], P(('rows', 'cols')), may hold values from 0 to 15, as said below
- counts: int32 [128], P(('rows', 'cols')), may hold values from 1 to 128, as said below
Outputs:
- scores: bfloat16 [16384, 256, 256], P(('rows', 'cols'))
- row_weights: float32 [32768], P('rows')
The draws below stay inside these ranges and needn't reach their ends.
Inputs may be any that keep to these rules, and one draw needn't show every extreme that they name: `requests`: each row lists 1 distinct local block indices. `pairs`: column 0 is below 8; column 1 is a fetch slot below 16. `counts`: slots at or beyond a device's count are padding.
All inputs are finite; a program needn't handle non-finite values.
Results may differ from the reference program's by a relative error of at most 0.0004.
Values may be sent and summed in bfloat16 or wider, within the bound.
No kernel may reach another device: no remote copies, remote signals or barrier semaphores. Data moves between devices by JAX's collectives and lax.ppermute only.
A program may use at most 128 MiB of HBM per device.

```python
import math
import jax
import jax.numpy as jnp
from jax import lax

D = 768
BLK = 256
QB_DEV = 8
CB_DEV = 8
FETCH = 1
P_DEV = 128
NQ = 32768
NC = 262144
NPAIRS = 16384
NREQ = 2048
N_ROWS = 16
N_COLS = 8
DEVICES = 128


def column_scales(key):
    return jnp.exp(jax.random.uniform(jax.random.fold_in(key, 7), (D,), jnp.float32, math.log(0.4), math.log(2.5)))


def embedding_draw(key, rows, tag):
    cols = column_scales(key)
    row_scale = jnp.exp(jax.random.uniform(jax.random.fold_in(key, tag), (rows, 1), jnp.float32, math.log(0.3), math.log(3.0)))
    base_key = jax.random.fold_in(key, tag + 1)
    base = jax.random.normal(base_key, (rows, D), jnp.float32)
    return (base * cols[None, :] * row_scale).astype(jnp.bfloat16)


def draw_queries(key, part):
    return embedding_draw(key, NQ, 21)


def draw_candidates(key, part):
    return embedding_draw(key, NC, 23)


def draw_requests(key, part):
    starts = jax.random.randint(jax.random.fold_in(key, 31), (NREQ,), 0, CB_DEV)
    shuffled = jax.random.permutation(jax.random.fold_in(key, 32), NREQ)
    starts = starts.at[shuffled[0]].set(CB_DEV - 1).at[shuffled[1]].set(0)
    steps_along = jnp.arange(FETCH, dtype=jnp.int32)
    return ((starts[:, None] + steps_along[None, :]) % CB_DEV).astype(jnp.int32)


def draw_pairs(key, part):
    query_block = jax.random.randint(jax.random.fold_in(key, 41), (NPAIRS,), 0, QB_DEV)
    fetch_slot = jax.random.randint(jax.random.fold_in(key, 42), (NPAIRS,), 0, N_ROWS * FETCH)
    shuffled = jax.random.permutation(jax.random.fold_in(key, 43), NPAIRS)
    query_block = query_block.at[shuffled[0]].set(QB_DEV - 1).at[shuffled[1]].set(0)
    fetch_slot = fetch_slot.at[shuffled[0]].set(N_ROWS * FETCH - 1).at[shuffled[1]].set(0)
    return jnp.stack([query_block, fetch_slot], axis=1).astype(jnp.int32)


def draw_counts(key, part):
    values = jax.random.randint(jax.random.fold_in(key, 51), (DEVICES,), P_DEV // 4, P_DEV + 1)
    shuffled = jax.random.permutation(jax.random.fold_in(key, 53), DEVICES)
    values = values.at[shuffled[0]].set(P_DEV).at[shuffled[1]].set(1)
    return values.astype(jnp.int32)


def setup_inputs(seed: int = 0) -> dict:
    streams_of = jax.random.split(jax.random.key(seed), 6)
    queries = draw_queries(jax.random.fold_in(streams_of[5], 71), 0)
    candidates = draw_candidates(jax.random.fold_in(streams_of[5], 71), 0)
    requests = draw_requests(jax.random.fold_in(streams_of[5], 71), 0)
    pairs = draw_pairs(jax.random.fold_in(streams_of[5], 71), 0)
    counts = draw_counts(jax.random.fold_in(streams_of[5], 71), 0)
    return {"queries": queries, "candidates": candidates, "requests": requests, "pairs": pairs, "counts": counts}


def inverse_norm(values):
    wide = values.astype(jnp.float32)
    return lax.rsqrt(lax.optimization_barrier(jnp.mean(wide * wide, axis=-1)) + 1e-06)

def reference(queries, candidates, requests, pairs, counts):
    inv_q = inverse_norm(queries)
    inv_c = inverse_norm(candidates)
    scale = 1.0 / math.sqrt(D)
    total = pairs.shape[0]
    slot_ids = jnp.arange(total, dtype=jnp.int32)
    device_of = slot_ids // P_DEV
    row_shard = device_of // N_COLS
    col_shard = device_of % N_COLS
    peer_row = pairs[:, 1] // FETCH
    position = pairs[:, 1] % FETCH
    local_id = requests[device_of * N_ROWS + peer_row, position]
    query_block = (row_shard * QB_DEV + pairs[:, 0]).astype(jnp.int32)
    cand_block = ((peer_row * N_COLS + col_shard) * CB_DEV + local_id).astype(jnp.int32)
    live_mask = (slot_ids % P_DEV < counts[device_of]).astype(jnp.float32)

    def take_rows(source, block_id):
        return lax.dynamic_slice_in_dim(source, (block_id * BLK).astype(jnp.int32), BLK, 0)

    def step(acc, group):
        qb = query_block[group]
        cb = cand_block[group]
        q_rows = jax.vmap(lambda block_id: take_rows(queries, block_id))(qb)
        c_rows = jax.vmap(lambda block_id: take_rows(candidates, block_id))(cb)
        q_inv = jax.vmap(lambda block_id: take_rows(inv_q, block_id))(qb)
        c_inv = jax.vmap(lambda block_id: take_rows(inv_c, block_id))(cb)
        dots = jnp.einsum('pid,pjd->pij', q_rows.astype(jnp.float32), c_rows.astype(jnp.float32), precision=lax.Precision.HIGHEST)
        zvals = dots * q_inv[:, :, None] * c_inv[:, None, :] * scale
        positive = jnp.maximum(zvals - 1.0, 0.0) * live_mask[group][:, None, None]
        acc = acc.at[qb].add(lax.optimization_barrier(jnp.sum(positive, axis=-1)))
        return (acc, positive.astype(jnp.bfloat16))
    groups = slot_ids.reshape(-1, 8)
    start_acc = jnp.zeros((NQ // BLK, BLK), jnp.float32)
    acc, tiles = lax.scan(step, start_acc, groups)
    scores = tiles.reshape(total, BLK, BLK)
    row_weights = acc.reshape(-1) / BLK
    return (scores, row_weights)
```

```python
import functools
import math

import jax
import jax.numpy as jnp
from jax import lax
from jax.experimental import pallas as pl
from jax.experimental.pallas import tpu as pltpu
from jax.sharding import PartitionSpec as P

BLK = 256
LANES = 128
RING = 4
ZRING = 16
WINDOW = 5
HEAD = 3
ORDER = (
    (1, 1), (3, 3), (1, 3), (3, 1), (2, 0), (0, 2), (2, 1), (0, 3),
    (2, 3), (0, 1), (1, 2), (3, 0), (3, 2), (1, 0), (2, 2),
)
CALLS = ((0, 4), (4, 8), (8, 12), (12, 15), (15, 16))


def inverse_norm(values):
    wide = values.astype(jnp.float32)
    return lax.rsqrt(jnp.mean(wide * wide, axis=-1) + 1e-06)


def pair_kernel(first, n_src, zero_fill, feature_dim, meta, *refs):
    q_hbm, iq_hbm = refs[:2]
    srcs = refs[2 : 2 + n_src]
    out, sums, q, iq, cbuf, ic, acc, ring, zero, qsem, iqsem, csem, osem, zsem = refs[-14:]
    n_pairs = out.shape[0]
    ranks_row = 3
    lo = meta[ranks_row, first]
    hi = meta[ranks_row, first + n_src]
    copies = []
    for i in range(n_src):
        copies.append(pltpu.make_async_copy(srcs[i], cbuf.at[i], csem.at[i]))
    q_copy = pltpu.make_async_copy(q_hbm, q, qsem)
    iq_copy = pltpu.make_async_copy(iq_hbm, iq, iqsem)
    copies[0].start()
    q_copy.start()
    iq_copy.start()
    for copy in copies[1:]:
        copy.start()
    acc[...] = jnp.zeros_like(acc)
    if zero_fill:
        zero[...] = jnp.zeros_like(zero)
        dead = meta[ranks_row, 16]

        def zero_copy(j):
            return pltpu.make_async_copy(
                zero, out.at[meta[0, j]], zsem.at[lax.rem(j - dead, ZRING)]
            )

        @pl.loop(dead, n_pairs)
        def _(j):
            @pl.when(j >= dead + ZRING)
            def _():
                zero_copy(j - ZRING).wait()

            zero_copy(j).start()

    ones = jnp.ones((8, feature_dim), jnp.bfloat16)
    dims = (((1,), (1,)), ((), ()))
    scale = 1.0 / math.sqrt(feature_dim)
    for i in range(n_src):
        copies[i].wait()
        wide = cbuf[i].astype(jnp.float32)
        square = wide * wide
        high = square.astype(jnp.bfloat16)
        low = (square - high.astype(jnp.float32)).astype(jnp.bfloat16)
        total = lax.dot_general(ones, high, dims, preferred_element_type=jnp.float32)
        total += lax.dot_general(ones, low, dims, preferred_element_type=jnp.float32)
        ic[i] = lax.rsqrt(total * (1.0 / feature_dim) + 1e-06) * scale
    q_copy.wait()
    iq_copy.wait()

    def score(j, slot, weight):
        qb = meta[1, j]
        c = meta[2, j] - first
        rows = pl.ds(pl.multiple_of(qb * BLK, BLK), BLK)
        dots = lax.dot_general(q[rows, :], cbuf[c], dims, preferred_element_type=jnp.float32)
        inv_q = iq[rows, :]
        inv_c = ic[c, 0:1, :]
        total = None
        for h in range(BLK // LANES):
            cols = slice(h * LANES, (h + 1) * LANES)
            pos = jnp.maximum(dots[:, cols] * inv_q * inv_c[:, cols] - 1.0, 0.0)
            ring[slot, :, cols] = pos.astype(jnp.bfloat16)
            total = pos if total is None else total + pos
        if weight is not None:
            total = total * weight
        acc[qb] += total

    def out_copy(j, slot):
        return pltpu.make_async_copy(ring.at[slot], out.at[meta[0, j]], osem.at[slot])

    half = RING // 2
    steps = (hi - lo + 1) // 2

    @pl.loop(0, steps)
    def _(i):
        slot = lax.rem(i, half) * 2
        a = lo + 2 * i
        b = jnp.minimum(a + 1, hi - 1)

        @pl.when(i >= half)
        def _():
            out_copy(a - RING, slot).wait()
            out_copy(a - RING + 1, slot + 1).wait()

        score(a, slot, None)
        score(b, slot + 1, (a + 1 < hi).astype(jnp.float32))
        out_copy(a, slot).start()

        @pl.when(a + 1 < hi)
        def _():
            out_copy(b, slot + 1).start()

    @pl.loop(jnp.maximum(lo, lo + 2 * (steps - half)), hi)
    def _(j):
        out_copy(j, lax.rem(j - lo, RING)).wait()

    if zero_fill:

        @pl.loop(jnp.maximum(dead, n_pairs - ZRING), n_pairs)
        def _(j):
            zero_copy(j).wait()

    sums[...] = jnp.sum(acc[...], axis=-1)


def take_kernel(codes, wanted, to, candidates, *refs):
    outs, sem = refs[:-1], refs[-1]
    copies = []
    for i, code in enumerate(codes):
        start = pl.multiple_of(wanted[to[code]] * BLK, BLK)
        copies.append(
            pltpu.make_async_copy(candidates.at[pl.ds(start, BLK)], outs[i], sem.at[i])
        )
    for copy in copies:
        copy.start()
    for copy in copies:
        copy.wait()


def take_blocks(offsets, wanted, to, candidates):
    side = math.isqrt(to.shape[0])
    smem = pl.BlockSpec(memory_space=pltpu.SMEM)
    hbm = pl.BlockSpec(memory_space=pl.ANY)
    codes = tuple(dy * side + dz for dy, dz in offsets)
    return list(
        pl.pallas_call(
            functools.partial(take_kernel, codes),
            out_shape=(
                jax.ShapeDtypeStruct((BLK, candidates.shape[1]), candidates.dtype),
            )
            * len(codes),
            in_specs=[smem, smem, pl.BlockSpec(memory_space=pltpu.HBM)],
            out_specs=(hbm,) * len(codes),
            scratch_shapes=[pltpu.SemaphoreType.DMA((len(codes),))],
            compiler_params=pltpu.CompilerParams(vmem_limit_bytes=1 << 20),
            name="take_%d" % len(codes),
        )(wanted, to, candidates)
    )


def score_pairs(first, sources, zero_fill, n_pairs, meta, queries, inv_q, *out):
    n_src = len(sources)
    feature_dim = queries.shape[1]
    q_rows = queries.shape[0]
    blocks = q_rows // BLK
    pairs_here = max(n_pairs * n_src // 16, 1)
    hbm = pl.BlockSpec(memory_space=pl.ANY)
    return pl.pallas_call(
        functools.partial(pair_kernel, first, n_src, zero_fill, feature_dim),
        out_shape=(
            jax.ShapeDtypeStruct((n_pairs, BLK, BLK), jnp.bfloat16),
            jax.ShapeDtypeStruct((blocks, BLK), jnp.float32),
        ),
        in_specs=[pl.BlockSpec(memory_space=pltpu.SMEM)] + [hbm] * (n_src + 2 + len(out)),
        out_specs=(hbm, pl.BlockSpec(memory_space=pltpu.VMEM)),
        scratch_shapes=[
            pltpu.VMEM((q_rows, feature_dim), jnp.bfloat16),
            pltpu.VMEM((q_rows, LANES), jnp.float32),
            pltpu.VMEM((n_src, BLK, feature_dim), jnp.bfloat16),
            pltpu.VMEM((n_src, 8, BLK), jnp.float32),
            pltpu.VMEM((blocks, BLK, LANES), jnp.float32),
            pltpu.VMEM((RING, BLK, BLK), jnp.bfloat16),
            pltpu.VMEM((BLK, BLK), jnp.bfloat16),
            pltpu.SemaphoreType.DMA,
            pltpu.SemaphoreType.DMA,
            pltpu.SemaphoreType.DMA((n_src,)),
            pltpu.SemaphoreType.DMA((RING,)),
            pltpu.SemaphoreType.DMA((ZRING,)),
        ],
        input_output_aliases={3 + n_src: 0} if out else {},
        cost_estimate=pl.CostEstimate(
            flops=2 * pairs_here * BLK * BLK * feature_dim,
            bytes_accessed=pairs_here * BLK * BLK * 2,
            transcendentals=0,
        ),
        compiler_params=pltpu.CompilerParams(vmem_limit_bytes=24 << 20),
        name="pairs_%d" % first,
    )(meta, queries, inv_q, *sources, *out)


def per_device(queries, candidates, requests, pairs, counts):
    row_count = lax.axis_size("rows")
    side = math.isqrt(row_count)
    col_count = lax.axis_size("cols")
    feature_dim = queries.shape[1]
    pair_count = pairs.shape[0]
    me = lax.axis_index("rows")
    my_y, my_z = me // side, me % side
    wanted = lax.all_to_all(requests, "rows", split_axis=0, concat_axis=0, tiled=True)[:, 0]

    offsets = ((0, 0),) + ORDER
    rank_of = [0] * row_count
    for rank, (dy, dz) in enumerate(offsets):
        rank_of[dy * side + dz] = rank
    slots = pairs[:, 1]
    away = ((my_y - slots // side) % side) * side + (my_z - slots % side) % side
    ids = jnp.arange(pair_count, dtype=jnp.int32)
    rank = jnp.zeros_like(slots)
    for code, value in enumerate(rank_of):
        rank = rank + jnp.where(away == code, value, 0)
    rank = jnp.where(ids < counts[0], rank, row_count)
    before = (rank[None, :] < rank[:, None]) | (
        (rank[None, :] == rank[:, None]) & (ids[None, :] < ids[:, None])
    )
    place = jnp.sum(before.astype(jnp.int32), axis=1)
    at = place[None, :] == ids[:, None]
    sorted_ids = jnp.sum(jnp.where(at, ids[None, :], 0), axis=1)
    sorted_q = jnp.sum(jnp.where(at, pairs[:, 0][None, :], 0), axis=1)
    sorted_rank = jnp.sum(jnp.where(at, rank[None, :], 0), axis=1)
    starts = jnp.sum((rank[None, :] < ids[:, None]).astype(jnp.int32), axis=1)
    meta = jnp.stack([sorted_ids, sorted_q, sorted_rank, starts])

    inv_q = jnp.broadcast_to(inverse_norm(queries)[:, None], (queries.shape[0], LANES))
    codes = jnp.arange(row_count, dtype=jnp.int32)
    to = ((my_y + codes // side) % side) * side + (my_z + codes % side) % side
    sends = take_blocks(ORDER[:HEAD], wanted, to, candidates)
    sends += take_blocks(ORDER[HEAD:] + ((0, 0),), wanted, to, candidates)
    arrived = [sends.pop()]
    out, local = None, None
    for k, (dy, dz) in enumerate(ORDER):
        send = sends[k]
        if k >= WINDOW:
            send, arrived[k - WINDOW + 1] = lax.optimization_barrier(
                (send, arrived[k - WINDOW + 1])
            )
        perm = [
            (y * side + z, ((y + dy) % side) * side + (z + dz) % side)
            for y in range(side)
            for z in range(side)
        ]
        arrived.append(lax.ppermute(send, "rows", perm))
    for call, (lo, hi) in enumerate(CALLS):
        out, sums = score_pairs(
            lo, arrived[lo:hi], call == 0, pair_count, meta, queries, inv_q,
            *(() if out is None else (out,)),
        )
        local = sums if local is None else local + sums
    totals = local.reshape(-1)
    step = 1
    while step < col_count:
        totals = totals + lax.ppermute(totals, "cols", [(i, i ^ step) for i in range(col_count)])
        step *= 2
    return out, totals * (1.0 / BLK)


def solution(mesh):
    in_specs = (
        P("rows", None),
        P(("rows", "cols"), None),
        P(("rows", "cols"), None),
        P(("rows", "cols"), None),
        P(("rows", "cols")),
    )
    out_specs = (P(("rows", "cols"), None, None), P("rows"))
    return jax.shard_map(
        per_device, mesh=mesh, in_specs=in_specs, out_specs=out_specs, check_vma=False
    )
```

```python
import math

import jax
import jax.numpy as jnp
from jax import lax
from jax.experimental import pallas as pl
from jax.experimental.pallas import tpu as pltpu
from jax.sharding import PartitionSpec as P

BLK = 256
LANES = 128
UNROLL = 8
TILES, LIVE = 0, 1


def inverse_norm(values):
    wide = values.astype(jnp.float32)
    return lax.rsqrt(jnp.mean(wide * wide, axis=-1) + 1e-06)


def pair_kernel(meta, q, iq, ic, fetched, out, sums, cbuf, acc, ring, zero, csem, osem):
    n_pairs = out.shape[0]
    n_src = cbuf.shape[0]
    depth = ring.shape[0]
    hi = meta[3, TILES]
    dead = meta[3, LIVE]

    def load(i):
        return pltpu.make_async_copy(fetched.at[pl.ds(i * BLK, BLK)], cbuf.at[i], csem.at[i])

    for i in range(n_src):
        load(i).start()
    zero[...] = jnp.zeros_like(zero)

    def zero_copy(j):
        return pltpu.make_async_copy(zero, out.at[meta[0, j]], osem.at[j])

    @pl.loop(dead, n_pairs)
    def _(j):
        zero_copy(j).start()

    acc[...] = jnp.zeros_like(acc)
    for i in range(n_src):
        load(i).wait()

    def score(t, slot, weight):
        qb = meta[1, t] % 8
        c = meta[1, t] // 8
        rows = pl.ds(pl.multiple_of(qb * BLK, BLK), BLK)
        dots = lax.dot_general(
            q[rows, :], cbuf[c], (((1,), (1,)), ((), ())), preferred_element_type=jnp.float32
        )
        inv_q = iq[rows, :]
        inv_c = ic[pl.ds(c, 1), :]
        total = None
        for h in range(BLK // LANES):
            cols = slice(h * LANES, (h + 1) * LANES)
            pos = jnp.maximum(dots[:, cols] * inv_q * inv_c[:, cols] - 1.0, 0.0)
            ring[slot, :, cols] = pos.astype(jnp.bfloat16)
            total = pos if total is None else total + pos
        acc[qb] += total * weight

    def tile_copies(t, slot, start):
        @pl.loop(meta[2, t], meta[2, t + 1])
        def _(j):
            copy = pltpu.make_async_copy(ring.at[slot], out.at[meta[0, j]], osem.at[j])
            copy.start() if start else copy.wait()

    rounds = depth // UNROLL
    steps = (hi + UNROLL - 1) // UNROLL

    @pl.loop(0, steps)
    def _(i):
        slot = lax.rem(i, rounds) * UNROLL
        a = UNROLL * i

        @pl.when(i >= rounds)
        def _():
            for u in range(UNROLL):
                tile_copies(a - depth + u, slot + u, False)

        for u in range(UNROLL):
            t = jnp.minimum(a + u, hi - 1)
            count = jnp.where(a + u < hi, meta[2, t + 1] - meta[2, t], 0)
            score(t, slot + u, count.astype(jnp.float32))
        for u in range(UNROLL):

            @pl.when(a + u < hi)
            def _():
                tile_copies(a + u, slot + u, True)

    for qb in range(acc.shape[0]):
        sums[qb : qb + 1, :] = jnp.sum(acc[qb].T, axis=0, keepdims=True)

    @pl.loop(jnp.maximum(0, UNROLL * (steps - rounds)), hi)
    def _(t):
        tile_copies(t, lax.rem(t, depth), False)

    @pl.loop(dead, n_pairs)
    def _(j):
        zero_copy(j).wait()


def score_pairs(n_pairs, meta, queries, inv_q, inv_c, fetched):
    n_src = fetched.shape[0] // BLK
    feature_dim = queries.shape[1]
    blocks = queries.shape[0] // BLK
    hbm = pl.BlockSpec(memory_space=pl.ANY)
    vmem = pl.BlockSpec(memory_space=pltpu.VMEM)
    return pl.pallas_call(
        pair_kernel,
        out_shape=(
            jax.ShapeDtypeStruct((n_pairs, BLK, BLK), jnp.bfloat16),
            jax.ShapeDtypeStruct((blocks, BLK), jnp.float32),
        ),
        in_specs=[pl.BlockSpec(memory_space=pltpu.SMEM), vmem, vmem, vmem, hbm],
        out_specs=(hbm, vmem),
        scratch_shapes=[
            pltpu.VMEM((n_src, BLK, feature_dim), jnp.bfloat16),
            pltpu.VMEM((blocks, BLK, LANES), jnp.float32),
            pltpu.VMEM((2 * UNROLL, BLK, BLK), jnp.bfloat16),
            pltpu.VMEM((BLK, BLK), jnp.bfloat16),
            pltpu.SemaphoreType.DMA((n_src,)),
            pltpu.SemaphoreType.DMA((n_pairs,)),
        ],
        cost_estimate=pl.CostEstimate(
            flops=2 * n_pairs * BLK * BLK * feature_dim,
            bytes_accessed=n_pairs * BLK * BLK * 2,
            transcendentals=0,
        ),
        compiler_params=pltpu.CompilerParams(vmem_limit_bytes=24 << 20),
        name="pairs",
    )(meta, queries, inv_q, inv_c, fetched)


def take_kernel(wanted, candidates, out, stage, sem):
    loads, stores = [], []
    for k in range(stage.shape[0]):
        block = candidates.at[pl.ds(pl.multiple_of(wanted[k] * BLK, BLK), BLK)]
        loads.append(pltpu.make_async_copy(block, stage.at[k], sem.at[0, k]))
        part = out.at[pl.ds(k * BLK, BLK)]
        stores.append(pltpu.make_async_copy(stage.at[k], part, sem.at[1, k]))
    for load in loads:
        load.start()
    for load, store in zip(loads, stores):
        load.wait()
        store.start()
    for store in stores:
        store.wait()


def take_blocks(wanted, candidates):
    count = wanted.shape[0]
    hbm = pl.BlockSpec(memory_space=pltpu.HBM)
    return pl.pallas_call(
        take_kernel,
        out_shape=pltpu.HBM((count * BLK, candidates.shape[1]), candidates.dtype),
        in_specs=[pl.BlockSpec(memory_space=pltpu.SMEM), hbm],
        out_specs=hbm,
        scratch_shapes=[
            pltpu.VMEM((count, BLK, candidates.shape[1]), candidates.dtype),
            pltpu.SemaphoreType.DMA((2, count)),
        ],
        compiler_params=pltpu.CompilerParams(vmem_limit_bytes=16 << 20),
        name="take",
    )(wanted, pltpu.with_memory_space_constraint(candidates, pltpu.HBM))


def per_device(queries, candidates, requests, pairs, counts):
    row_count = lax.axis_size("rows")
    col_count = lax.axis_size("cols")
    feature_dim = queries.shape[1]
    pair_count = pairs.shape[0]
    wanted = lax.all_to_all(requests, "rows", split_axis=0, concat_axis=0, tiled=True)[:, 0]
    sends = take_blocks(wanted, candidates)
    fetched = lax.all_to_all(sends, "rows", split_axis=0, concat_axis=0, tiled=True)
    queries, candidates, pairs, sends = lax.optimization_barrier(
        (queries, candidates, pairs, sends)
    )

    ids = jnp.arange(pair_count, dtype=jnp.int32)
    key = jnp.where(ids < counts[0], pairs[:, 1] * 8 + pairs[:, 0], row_count * 8)
    less = key[None, :] < key[:, None]
    twin = (key[None, :] == key[:, None]) & (ids[None, :] < ids[:, None])
    place = jnp.sum((less | twin).astype(jnp.int32), axis=1)
    lead = jnp.logical_not(jnp.any(twin, axis=1))
    tile = jnp.sum((less & lead[None, :]).astype(jnp.int32), axis=1)
    wide = jnp.arange(2 * pair_count, dtype=jnp.int32)
    at = place[None, :] == wide[:, None]
    sorted_ids = jnp.sum(jnp.where(at, ids[None, :], 0), axis=1)
    at = lead[None, :] & (tile[None, :] == wide[:, None])
    tile_key = jnp.sum(jnp.where(at, (key % (row_count * 8))[None, :], 0), axis=1)
    first_pair = jnp.sum(jnp.where(at, (place - pair_count)[None, :], 0), axis=1) + pair_count
    tiles = jnp.sum((lead & (ids < counts[0])).astype(jnp.int32))
    ends = jnp.where(wide == TILES, tiles, counts[0])
    meta = jnp.stack([sorted_ids, tile_key, first_pair, ends])

    inv_q = jnp.broadcast_to(inverse_norm(queries)[:, None], (queries.shape[0], LANES))
    norms = inverse_norm(candidates.reshape(-1, BLK, feature_dim)) * (1.0 / math.sqrt(feature_dim))
    norms = lax.all_gather(norms, "rows", axis=0, tiled=False)
    picked = requests == jnp.arange(norms.shape[1], dtype=jnp.int32)[None, :]
    inv_c = jnp.sum(jnp.where(picked[:, :, None], norms, 0.0), axis=1)

    out, local = score_pairs(pair_count, meta, queries, inv_q, inv_c, fetched)
    totals = local.reshape(-1)
    step = 1
    while step < col_count:
        totals = totals + lax.ppermute(totals, "cols", [(i, i ^ step) for i in range(col_count)])
        step *= 2
    return out, totals * (1.0 / BLK)


def solution(mesh):
    in_specs = (
        P("rows", None),
        P(("rows", "cols"), None),
        P(("rows", "cols"), None),
        P(("rows", "cols"), None),
        P(("rows", "cols")),
    )
    out_specs = (P(("rows", "cols"), None, None), P("rows"))
    return jax.shard_map(
        per_device, mesh=mesh, in_specs=in_specs, out_specs=out_specs, check_vma=False
    )
```

```python
import functools
import math

import jax
import jax.numpy as jnp
from jax import lax
from jax.experimental import pallas as pl
from jax.experimental.pallas import tpu as pltpu
from jax.sharding import PartitionSpec as P

BLK = 256
LANES = 128
CALL_LIMIT = 32
HEAD = 5
ORDER = (
    (1, 1), (3, 3), (1, 3), (3, 1), (2, 0), (0, 2), (2, 1), (0, 3),
    (2, 3), (0, 1), (1, 2), (3, 0), (3, 2), (1, 0), (2, 2),
)
CALLS = ((0, 7, 8, 11), (7, 11, 8, 15), (11, 14, 8, 15), (14, 16, 4, 15))


def inverse_norm(values):
    wide = values.astype(jnp.float32)
    return lax.rsqrt(jnp.mean(wide * wide, axis=-1) + 1e-06)


def pair_kernel(call, n_src, unroll, zero_fill, feature_dim, meta, q, iq, *refs):
    srcs = refs[:n_src]
    out, sums, cbuf, ic, acc, ring, zero, csem, osem = refs[-9:]
    n_pairs = out.shape[0]
    depth = ring.shape[0]
    lo = meta[3, call]
    hi = meta[3, call + 1]
    copies = [pltpu.make_async_copy(srcs[i], cbuf.at[i], csem.at[i]) for i in range(n_src)]
    for copy in copies:
        copy.start()
    acc[...] = jnp.zeros_like(acc)
    if zero_fill:
        zero[...] = jnp.zeros_like(zero)
        dead = meta[3, CALL_LIMIT]

        def zero_copy(j):
            return pltpu.make_async_copy(zero, out.at[meta[0, j]], osem.at[j])

        @pl.loop(dead, n_pairs)
        def _(j):
            zero_copy(j).start()

    dims = (((1,), (1,)), ((), ()))
    scale = 1.0 / math.sqrt(feature_dim)
    for i in range(n_src):
        copies[i].wait()
        squares = None
        for h in range(feature_dim // LANES):
            wide = cbuf[i, :, h * LANES : (h + 1) * LANES].astype(jnp.float32)
            squares = wide * wide if squares is None else squares + wide * wide
        total = jnp.sum(squares.T, axis=0, keepdims=True)
        ic[i] = lax.rsqrt(total * (1.0 / feature_dim) + 1e-06) * scale

    def score(t, slot, weight):
        qb = meta[1, t] % 8
        c = meta[1, t] // 8
        rows = pl.ds(pl.multiple_of(qb * BLK, BLK), BLK)
        dots = lax.dot_general(q[rows, :], cbuf[c], dims, preferred_element_type=jnp.float32)
        inv_q = iq[rows, :]
        inv_c = ic[c]
        total = None
        for h in range(BLK // LANES):
            cols = slice(h * LANES, (h + 1) * LANES)
            pos = jnp.maximum(dots[:, cols] * inv_q * inv_c[:, cols] - 1.0, 0.0)
            ring[slot, :, cols] = pos.astype(jnp.bfloat16)
            total = pos if total is None else total + pos
        acc[qb] += total * weight

    def tile_copies(t, slot, start):
        @pl.loop(meta[2, t], meta[2, t + 1])
        def _(j):
            copy = pltpu.make_async_copy(ring.at[slot], out.at[meta[0, j]], osem.at[j])
            copy.start() if start else copy.wait()

    rounds = depth // unroll
    steps = (hi - lo + unroll - 1) // unroll

    @pl.loop(0, steps)
    def _(i):
        slot = lax.rem(i, rounds) * unroll
        a = lo + unroll * i

        @pl.when(i >= rounds)
        def _():
            for u in range(unroll):
                tile_copies(a - depth + u, slot + u, False)

        for u in range(unroll):
            t = jnp.minimum(a + u, hi - 1)
            count = jnp.where(a + u < hi, meta[2, t + 1] - meta[2, t], 0)
            score(t, slot + u, count.astype(jnp.float32))
        for u in range(unroll):

            @pl.when(a + u < hi)
            def _():
                tile_copies(a + u, slot + u, True)

    @pl.loop(jnp.maximum(lo, lo + unroll * (steps - rounds)), hi)
    def _(t):
        tile_copies(t, lax.rem(t - lo, depth), False)

    if zero_fill:

        @pl.loop(dead, n_pairs)
        def _(j):
            zero_copy(j).wait()

    for qb in range(acc.shape[0]):
        sums[qb : qb + 1, :] = jnp.sum(acc[qb].T, axis=0, keepdims=True)


def take_kernel(codes, wanted, to, candidates, *refs):
    outs, sem = refs[:-1], refs[-1]
    copies = []
    for i, code in enumerate(codes):
        start = pl.multiple_of(wanted[to[code]] * BLK, BLK)
        copies.append(
            pltpu.make_async_copy(candidates.at[pl.ds(start, BLK)], outs[i], sem.at[i])
        )
    for copy in copies:
        copy.start()
    for copy in copies:
        copy.wait()


def take_blocks(offsets, wanted, to, candidates):
    side = math.isqrt(to.shape[0])
    smem = pl.BlockSpec(memory_space=pltpu.SMEM)
    hbm = pl.BlockSpec(memory_space=pl.ANY)
    codes = tuple(dy * side + dz for dy, dz in offsets)
    return list(
        pl.pallas_call(
            functools.partial(take_kernel, codes),
            out_shape=(
                jax.ShapeDtypeStruct((BLK, candidates.shape[1]), candidates.dtype),
            )
            * len(codes),
            in_specs=[smem, smem, pl.BlockSpec(memory_space=pltpu.HBM)],
            out_specs=(hbm,) * len(codes),
            scratch_shapes=[pltpu.SemaphoreType.DMA((len(codes),))],
            compiler_params=pltpu.CompilerParams(vmem_limit_bytes=1 << 20),
            name="take_%d" % len(codes),
        )(wanted, to, pltpu.with_memory_space_constraint(candidates, pltpu.HBM))
    )


def score_pairs(call, unroll, sources, zero_fill, n_pairs, meta, queries, inv_q, *out):
    n_src = len(sources)
    feature_dim = queries.shape[1]
    blocks = queries.shape[0] // BLK
    pairs_here = max(n_pairs * n_src // 16, 1)
    hbm = pl.BlockSpec(memory_space=pl.ANY)
    vmem = pl.BlockSpec(memory_space=pltpu.VMEM)
    return pl.pallas_call(
        functools.partial(pair_kernel, call, n_src, unroll, zero_fill, feature_dim),
        out_shape=(
            jax.ShapeDtypeStruct((n_pairs, BLK, BLK), jnp.bfloat16),
            jax.ShapeDtypeStruct((blocks, BLK), jnp.float32),
        ),
        in_specs=[pl.BlockSpec(memory_space=pltpu.SMEM), vmem, vmem]
        + [hbm] * (n_src + len(out)),
        out_specs=(hbm, vmem),
        scratch_shapes=[
            pltpu.VMEM((n_src, BLK, feature_dim), jnp.bfloat16),
            pltpu.VMEM((n_src, 1, BLK), jnp.float32),
            pltpu.VMEM((blocks, BLK, LANES), jnp.float32),
            pltpu.VMEM((2 * unroll, BLK, BLK), jnp.bfloat16),
            pltpu.VMEM((BLK, BLK), jnp.bfloat16),
            pltpu.SemaphoreType.DMA((n_src,)),
            pltpu.SemaphoreType.DMA((n_pairs,)),
        ],
        input_output_aliases={3 + n_src: 0} if out else {},
        cost_estimate=pl.CostEstimate(
            flops=2 * pairs_here * BLK * BLK * feature_dim,
            bytes_accessed=pairs_here * BLK * BLK * 2,
            transcendentals=0,
        ),
        compiler_params=pltpu.CompilerParams(vmem_limit_bytes=12 << 20),
        name="pairs_%d" % call,
    )(meta, queries, inv_q, *sources, *out)


def per_device(queries, candidates, requests, pairs, counts):
    row_count = lax.axis_size("rows")
    side = math.isqrt(row_count)
    col_count = lax.axis_size("cols")
    feature_dim = queries.shape[1]
    pair_count = pairs.shape[0]
    me = lax.axis_index("rows")
    my_y, my_z = me // side, me % side
    wanted = lax.all_to_all(requests, "rows", split_axis=0, concat_axis=0, tiled=True)[:, 0]

    offsets = ((0, 0),) + ORDER
    key_of = [0] * row_count
    for call, (lo, hi, _, _) in enumerate(CALLS):
        for rank in range(lo, hi):
            dy, dz = offsets[rank]
            key_of[dy * side + dz] = (call * row_count + rank - lo) * 8
    slots = pairs[:, 1]
    away = ((my_y - slots // side) % side) * side + (my_z - slots % side) % side
    ids = jnp.arange(pair_count, dtype=jnp.int32)
    key = pairs[:, 0]
    for code, value in enumerate(key_of):
        key = key + jnp.where(away == code, value, 0)
    key = jnp.where(ids < counts[0], key, CALL_LIMIT * row_count * 8)
    less = key[None, :] < key[:, None]
    twin = (key[None, :] == key[:, None]) & (ids[None, :] < ids[:, None])
    place = jnp.sum((less | twin).astype(jnp.int32), axis=1)
    lead = jnp.logical_not(jnp.any(twin, axis=1))
    tile = jnp.sum((less & lead[None, :]).astype(jnp.int32), axis=1)
    wide = jnp.arange(2 * pair_count, dtype=jnp.int32)
    at = place[None, :] == wide[:, None]
    sorted_ids = jnp.sum(jnp.where(at, ids[None, :], 0), axis=1)
    at = lead[None, :] & (tile[None, :] == wide[:, None])
    tile_key = jnp.sum(jnp.where(at, (key % (row_count * 8))[None, :], 0), axis=1)
    first_pair = jnp.sum(jnp.where(at, (place - pair_count)[None, :], 0), axis=1) + pair_count
    below = lead[None, :] & (key[None, :] < (wide * (row_count * 8))[:, None])
    starts = jnp.sum(below.astype(jnp.int32), axis=1)
    starts = jnp.where(wide == CALL_LIMIT, counts[0], starts)
    meta = jnp.stack([sorted_ids, tile_key, first_pair, starts])

    codes = jnp.arange(row_count, dtype=jnp.int32)
    to = ((my_y + codes // side) % side) * side + (my_z + codes % side) % side
    sends = take_blocks(ORDER[:HEAD], wanted, to, candidates)
    arrived = [None]
    out, sums, scored = None, [], 0

    def score(out, scored):
        lo, hi, unroll, _ = CALLS[scored]
        out, part = score_pairs(
            scored, unroll, arrived[lo:hi], scored == 0, pair_count, meta, queries, inv_q,
            *(() if out is None else (out,)),
        )
        sums.append(part)
        return out

    for k, (dy, dz) in enumerate(ORDER):
        if k == HEAD:
            to = lax.optimization_barrier((to, arrived[1]))[0]
            sends += take_blocks(ORDER[HEAD:] + ((0, 0),), wanted, to, candidates)
            arrived[0] = sends.pop()
            inv_q = inverse_norm(lax.optimization_barrier((queries, arrived[1]))[0])
            inv_q = jnp.broadcast_to(inv_q[:, None], (queries.shape[0], LANES))
        send = sends[k]
        if scored < len(CALLS) and CALLS[scored][3] == k:
            out = score(out, scored)
            scored += 1
        if sums:
            send = lax.optimization_barrier((send, sums[-1]))[0]
        perm = [
            (y * side + z, ((y + dy) % side) * side + (z + dz) % side)
            for y in range(side)
            for z in range(side)
        ]
        arrived.append(lax.ppermute(send, "rows", perm))
    while scored < len(CALLS):
        out = score(out, scored)
        scored += 1
    local = functools.reduce(jnp.add, sums)
    totals = local.reshape(-1)

    def other(values, flip):
        return lax.ppermute(values, "cols", [(i, i ^ flip) for i in range(col_count)])

    totals = totals + other(totals, 1)
    totals = (totals + other(totals, 2)) + (other(totals, 4) + other(totals, 6))
    return out, totals * (1.0 / BLK)


def solution(mesh):
    in_specs = (
        P("rows", None),
        P(("rows", "cols"), None),
        P(("rows", "cols"), None),
        P(("rows", "cols"), None),
        P(("rows", "cols")),
    )
    out_specs = (P(("rows", "cols"), None, None), P("rows"))
    return jax.shard_map(
        per_device, mesh=mesh, in_specs=in_specs, out_specs=out_specs, check_vma=False
    )
```

```python
import functools
import math

import jax
import jax.numpy as jnp
from jax import lax
from jax.experimental import pallas as pl
from jax.experimental.pallas import tpu as pltpu
from jax.sharding import PartitionSpec as P

BLK = 256
LANES = 128
CALL_LIMIT = 32
HEAD = 5
PAIRED = (
    ((1, 1), (3, 3)), ((3, 3), (1, 1)), ((1, 3), (3, 1)), ((3, 1), (1, 3)), ((2, 0), (0, 2)),
    ((0, 2), (2, 0)), ((2, 1), (0, 3)), ((0, 3), (2, 1)), ((2, 3), (0, 1)), ((0, 1), (2, 3)),
    ((1, 2), (3, 0)), ((3, 0), (1, 2)), ((3, 2), (1, 0)), ((1, 0), (3, 2)), ((2, 2), (2, 2)),
)
CALLS = ((0, 7, 8, 11), (7, 11, 8, 15), (11, 15, 8, 15), (15, 16, 4, 15))


def inverse_norm(values):
    wide = values.astype(jnp.float32)
    return lax.rsqrt(jnp.mean(wide * wide, axis=-1) + 1e-06)


def pair_kernel(call, n_src, unroll, zero_fill, feature_dim, meta, q, iq, *refs):
    srcs = refs[:n_src]
    out, sums, cbuf, ic, acc, ring, zero, csem, osem = refs[-9:]
    n_pairs = out.shape[0]
    depth = ring.shape[0]
    lo = meta[3, call]
    hi = meta[3, call + 1]
    copies = [pltpu.make_async_copy(srcs[i], cbuf.at[i], csem.at[i]) for i in range(n_src)]
    for copy in copies:
        copy.start()
    acc[...] = jnp.zeros_like(acc)
    if zero_fill:
        zero[...] = jnp.zeros_like(zero)
        dead = meta[3, CALL_LIMIT]

        def zero_copy(j):
            return pltpu.make_async_copy(zero, out.at[meta[0, j]], osem.at[j])

        @pl.loop(dead, n_pairs)
        def _(j):
            zero_copy(j).start()

    dims = (((1,), (1,)), ((), ()))
    scale = 1.0 / math.sqrt(feature_dim)
    for i in range(n_src):
        copies[i].wait()
        squares = None
        for h in range(feature_dim // LANES):
            wide = cbuf[i, :, h * LANES : (h + 1) * LANES].astype(jnp.float32)
            squares = wide * wide if squares is None else squares + wide * wide
        total = jnp.sum(squares.T, axis=0, keepdims=True)
        ic[i] = lax.rsqrt(total * (1.0 / feature_dim) + 1e-06) * scale

    def score(t, slot, weight):
        qb = meta[1, t] % 8
        c = meta[1, t] // 8
        rows = pl.ds(pl.multiple_of(qb * BLK, BLK), BLK)
        dots = lax.dot_general(q[rows, :], cbuf[c], dims, preferred_element_type=jnp.float32)
        inv_q = iq[rows, :]
        inv_c = ic[c]
        total = None
        for h in range(BLK // LANES):
            cols = slice(h * LANES, (h + 1) * LANES)
            pos = jnp.maximum(dots[:, cols] * inv_q * inv_c[:, cols] - 1.0, 0.0)
            ring[slot, :, cols] = pos.astype(jnp.bfloat16)
            total = pos if total is None else total + pos
        acc[qb] += total * weight

    def tile_copies(t, slot, start):
        @pl.loop(meta[2, t], meta[2, t + 1])
        def _(j):
            copy = pltpu.make_async_copy(ring.at[slot], out.at[meta[0, j]], osem.at[j])
            copy.start() if start else copy.wait()

    rounds = depth // unroll
    steps = (hi - lo + unroll - 1) // unroll

    @pl.loop(0, steps)
    def _(i):
        slot = lax.rem(i, rounds) * unroll
        a = lo + unroll * i

        @pl.when(i >= rounds)
        def _():
            for u in range(unroll):
                tile_copies(a - depth + u, slot + u, False)

        for u in range(unroll):
            t = jnp.minimum(a + u, hi - 1)
            count = jnp.where(a + u < hi, meta[2, t + 1] - meta[2, t], 0)
            score(t, slot + u, count.astype(jnp.float32))
        for u in range(unroll):

            @pl.when(a + u < hi)
            def _():
                tile_copies(a + u, slot + u, True)

    @pl.loop(jnp.maximum(lo, lo + unroll * (steps - rounds)), hi)
    def _(t):
        tile_copies(t, lax.rem(t - lo, depth), False)

    if zero_fill:

        @pl.loop(dead, n_pairs)
        def _(j):
            zero_copy(j).wait()

    for qb in range(acc.shape[0]):
        sums[qb : qb + 1, :] = jnp.sum(acc[qb].T, axis=0, keepdims=True)


def take_kernel(places, wanted, to, candidates, *refs):
    outs, sem = refs[:-1], refs[-1]
    copies = []
    for i, place in enumerate(places):
        start = pl.multiple_of(wanted[to[place]] * BLK, BLK)
        copies.append(
            pltpu.make_async_copy(candidates.at[pl.ds(start, BLK)], outs[i], sem.at[i])
        )
    for copy in copies:
        copy.start()
    for copy in copies:
        copy.wait()


def take_blocks(places, wanted, to, candidates):
    smem = pl.BlockSpec(memory_space=pltpu.SMEM)
    hbm = pl.BlockSpec(memory_space=pl.ANY)
    return list(
        pl.pallas_call(
            functools.partial(take_kernel, tuple(places)),
            out_shape=(
                jax.ShapeDtypeStruct((BLK, candidates.shape[1]), candidates.dtype),
            )
            * len(places),
            in_specs=[smem, smem, pl.BlockSpec(memory_space=pltpu.HBM)],
            out_specs=(hbm,) * len(places),
            scratch_shapes=[pltpu.SemaphoreType.DMA((len(places),))],
            compiler_params=pltpu.CompilerParams(vmem_limit_bytes=1 << 20),
            name="take_%d" % len(places),
        )(wanted, to, pltpu.with_memory_space_constraint(candidates, pltpu.HBM))
    )


def score_pairs(call, unroll, sources, zero_fill, n_pairs, meta, queries, inv_q, *out):
    n_src = len(sources)
    feature_dim = queries.shape[1]
    blocks = queries.shape[0] // BLK
    pairs_here = max(n_pairs * n_src // 16, 1)
    hbm = pl.BlockSpec(memory_space=pl.ANY)
    vmem = pl.BlockSpec(memory_space=pltpu.VMEM)
    return pl.pallas_call(
        functools.partial(pair_kernel, call, n_src, unroll, zero_fill, feature_dim),
        out_shape=(
            jax.ShapeDtypeStruct((n_pairs, BLK, BLK), jnp.bfloat16),
            jax.ShapeDtypeStruct((blocks, BLK), jnp.float32),
        ),
        in_specs=[pl.BlockSpec(memory_space=pltpu.SMEM), vmem, vmem]
        + [hbm] * (n_src + len(out)),
        out_specs=(hbm, vmem),
        scratch_shapes=[
            pltpu.VMEM((n_src, BLK, feature_dim), jnp.bfloat16),
            pltpu.VMEM((n_src, 1, BLK), jnp.float32),
            pltpu.VMEM((blocks, BLK, LANES), jnp.float32),
            pltpu.VMEM((2 * unroll, BLK, BLK), jnp.bfloat16),
            pltpu.VMEM((BLK, BLK), jnp.bfloat16),
            pltpu.SemaphoreType.DMA((n_src,)),
            pltpu.SemaphoreType.DMA((n_pairs,)),
        ],
        input_output_aliases={3 + n_src: 0} if out else {},
        cost_estimate=pl.CostEstimate(
            flops=2 * pairs_here * BLK * BLK * feature_dim,
            bytes_accessed=pairs_here * BLK * BLK * 2,
            transcendentals=0,
        ),
        compiler_params=pltpu.CompilerParams(vmem_limit_bytes=12 << 20),
        name="pairs_%d" % call,
    )(meta, queries, inv_q, *sources, *out)


def per_device(queries, candidates, requests, pairs, counts):
    row_count = lax.axis_size("rows")
    side = math.isqrt(row_count)
    col_count = lax.axis_size("cols")
    feature_dim = queries.shape[1]
    pair_count = pairs.shape[0]
    me = lax.axis_index("rows")
    my_y, my_z = me // side, me % side
    wanted = lax.all_to_all(requests, "rows", split_axis=0, concat_axis=0, tiled=True)[:, 0]

    odd = lax.axis_index("cols") % 2
    keys_of = []
    for parity in range(2):
        keys_of.append([0] * row_count)
        for call, (lo, hi, _, _) in enumerate(CALLS):
            for rank in range(lo, hi):
                dy, dz = PAIRED[rank - 1][parity] if rank else (0, 0)
                keys_of[parity][dy * side + dz] = (call * row_count + rank - lo) * 8
    slots = pairs[:, 1]
    away = ((my_y - slots // side) % side) * side + (my_z - slots % side) % side
    ids = jnp.arange(pair_count, dtype=jnp.int32)
    key = pairs[:, 0]
    for code, values in enumerate(zip(*keys_of)):
        key = key + jnp.where(away == code, jnp.where(odd == 1, values[1], values[0]), 0)
    key = jnp.where(ids < counts[0], key, CALL_LIMIT * row_count * 8)
    less = key[None, :] < key[:, None]
    twin = (key[None, :] == key[:, None]) & (ids[None, :] < ids[:, None])
    place = jnp.sum((less | twin).astype(jnp.int32), axis=1)
    lead = jnp.logical_not(jnp.any(twin, axis=1))
    tile = jnp.sum((less & lead[None, :]).astype(jnp.int32), axis=1)
    wide = jnp.arange(2 * pair_count, dtype=jnp.int32)
    at = place[None, :] == wide[:, None]
    sorted_ids = jnp.sum(jnp.where(at, ids[None, :], 0), axis=1)
    at = lead[None, :] & (tile[None, :] == wide[:, None])
    tile_key = jnp.sum(jnp.where(at, (key % (row_count * 8))[None, :], 0), axis=1)
    first_pair = jnp.sum(jnp.where(at, (place - pair_count)[None, :], 0), axis=1) + pair_count
    below = lead[None, :] & (key[None, :] < (wide * (row_count * 8))[:, None])
    starts = jnp.sum(below.astype(jnp.int32), axis=1)
    starts = jnp.where(wide == CALL_LIMIT, counts[0], starts)
    meta = jnp.stack([sorted_ids, tile_key, first_pair, starts])

    along = [
        [jnp.array([step[parity][axis] for step in PAIRED] + [0], jnp.int32) for axis in (0, 1)]
        for parity in (0, 1)
    ]
    dys, dzs = (jnp.where(odd == 1, along[1][axis], along[0][axis]) for axis in (0, 1))
    to = ((my_y + dys) % side) * side + (my_z + dzs) % side
    sends = take_blocks(range(HEAD), wanted, to, candidates)
    arrived = [None]
    out, sums, scored = None, [], 0

    def score(out, scored):
        lo, hi, unroll, _ = CALLS[scored]
        out, part = score_pairs(
            scored, unroll, arrived[lo:hi], scored == 0, pair_count, meta, queries, inv_q,
            *(() if out is None else (out,)),
        )
        sums.append(part)
        return out

    for k, step in enumerate(PAIRED):
        if k == HEAD:
            to = lax.optimization_barrier((to, arrived[1]))[0]
            sends += take_blocks(range(HEAD, row_count), wanted, to, candidates)
            arrived[0] = sends.pop()
            inv_q = inverse_norm(lax.optimization_barrier((queries, arrived[1]))[0])
            inv_q = jnp.broadcast_to(inv_q[:, None], (queries.shape[0], LANES))
        send = sends[k]
        if scored < len(CALLS) and CALLS[scored][3] == k:
            out = score(out, scored)
            scored += 1
        if sums:
            send = lax.optimization_barrier((send, sums[-1]))[0]
        perm = []
        for y in range(side):
            for z in range(side):
                for col in range(col_count):
                    dy, dz = step[col % 2]
                    target = ((y + dy) % side) * side + (z + dz) % side
                    perm.append(((y * side + z) * col_count + col, target * col_count + col))
        arrived.append(lax.ppermute(send, ("rows", "cols"), perm))
    while scored < len(CALLS):
        out = score(out, scored)
        scored += 1
    local = functools.reduce(jnp.add, sums)
    totals = local.reshape(-1)

    def other(values, flip):
        return lax.ppermute(values, "cols", [(i, i ^ flip) for i in range(col_count)])

    totals = totals + other(totals, 1)
    totals = (totals + other(totals, 2)) + (other(totals, 4) + other(totals, 6))
    return out, totals * (1.0 / BLK)


def solution(mesh):
    in_specs = (
        P("rows", None),
        P(("rows", "cols"), None),
        P(("rows", "cols"), None),
        P(("rows", "cols"), None),
        P(("rows", "cols")),
    )
    out_specs = (P(("rows", "cols"), None, None), P("rows"))
    return jax.shard_map(
        per_device, mesh=mesh, in_specs=in_specs, out_specs=out_specs, check_vma=False
    )
```

```python
import functools
import math

import jax
import jax.numpy as jnp
from jax import lax
from jax.experimental import pallas as pl
from jax.experimental.pallas import tpu as pltpu
from jax.sharding import PartitionSpec as P

BLK = 256
LANES = 128
CALL_LIMIT = 32
HEAD = 6
PAIRED = (
    ((1, 1), (3, 3)), ((3, 3), (1, 1)), ((1, 3), (3, 1)), ((3, 1), (1, 3)), ((2, 0), (0, 2)),
    ((0, 2), (2, 0)), ((2, 1), (0, 3)), ((0, 3), (2, 1)), ((2, 3), (0, 1)), ((0, 1), (2, 3)),
    ((1, 2), (3, 0)), ((3, 0), (1, 2)), ((3, 2), (1, 0)), ((1, 0), (3, 2)), ((2, 2), (2, 2)),
)
CALLS = ((0, 7, 8, 11), (7, 11, 8, 15), (11, 15, 8, 15), (15, 16, 4, 15))


def inverse_norm(values):
    wide = values.astype(jnp.float32)
    return lax.rsqrt(jnp.mean(wide * wide, axis=-1) + 1e-06)


def pair_kernel(call, n_src, unroll, zero_fill, feature_dim, meta, q, iq, *refs):
    srcs = refs[:n_src]
    out, sums, cbuf, ic, acc, ring, zero, csem, osem = refs[-9:]
    n_pairs = out.shape[0]
    depth = ring.shape[0]
    lo = meta[3, call]
    hi = meta[3, call + 1]
    copies = [pltpu.make_async_copy(srcs[i], cbuf.at[i], csem.at[i]) for i in range(n_src)]
    for copy in copies:
        copy.start()
    acc[...] = jnp.zeros_like(acc)
    if zero_fill:
        zero[...] = jnp.zeros_like(zero)
        dead = meta[3, CALL_LIMIT]

        def zero_copy(j):
            return pltpu.make_async_copy(zero, out.at[meta[0, j]], osem.at[j])

        @pl.loop(dead, n_pairs)
        def _(j):
            zero_copy(j).start()

    dims = (((1,), (1,)), ((), ()))
    scale = 1.0 / math.sqrt(feature_dim)
    for i in range(n_src):
        copies[i].wait()
        squares = None
        for h in range(feature_dim // LANES):
            wide = cbuf[i, :, h * LANES : (h + 1) * LANES].astype(jnp.float32)
            squares = wide * wide if squares is None else squares + wide * wide
        total = jnp.sum(squares.T, axis=0, keepdims=True)
        ic[i] = lax.rsqrt(total * (1.0 / feature_dim) + 1e-06) * scale

    def score(t, slot, weight):
        qb = meta[1, t] % 8
        c = meta[1, t] // 8
        rows = pl.ds(pl.multiple_of(qb * BLK, BLK), BLK)
        dots = lax.dot_general(q[rows, :], cbuf[c], dims, preferred_element_type=jnp.float32)
        inv_q = iq[rows, :]
        inv_c = ic[c]
        total = None
        for h in range(BLK // LANES):
            cols = slice(h * LANES, (h + 1) * LANES)
            pos = jnp.maximum(dots[:, cols] * inv_q * inv_c[:, cols] - 1.0, 0.0)
            ring[slot, :, cols] = pos.astype(jnp.bfloat16)
            total = pos if total is None else total + pos
        acc[qb] += total * weight

    def tile_copies(t, slot, start):
        @pl.loop(meta[2, t], meta[2, t + 1])
        def _(j):
            copy = pltpu.make_async_copy(ring.at[slot], out.at[meta[0, j]], osem.at[j])
            copy.start() if start else copy.wait()

    rounds = depth // unroll
    steps = (hi - lo + unroll - 1) // unroll

    @pl.loop(0, steps)
    def _(i):
        slot = lax.rem(i, rounds) * unroll
        a = lo + unroll * i

        @pl.when(i >= rounds)
        def _():
            for u in range(unroll):
                tile_copies(a - depth + u, slot + u, False)

        for u in range(unroll):
            t = jnp.minimum(a + u, hi - 1)
            count = jnp.where(a + u < hi, meta[2, t + 1] - meta[2, t], 0)
            score(t, slot + u, count.astype(jnp.float32))
        for u in range(unroll):

            @pl.when(a + u < hi)
            def _():
                tile_copies(a + u, slot + u, True)

    @pl.loop(jnp.maximum(lo, lo + unroll * (steps - rounds)), hi)
    def _(t):
        tile_copies(t, lax.rem(t - lo, depth), False)

    if zero_fill:

        @pl.loop(dead, n_pairs)
        def _(j):
            zero_copy(j).wait()

    for qb in range(acc.shape[0]):
        sums[qb : qb + 1, :] = jnp.sum(acc[qb].T, axis=0, keepdims=True)


def take_kernel(places, wanted, to, candidates, *refs):
    outs, sem = refs[:-1], refs[-1]
    copies = []
    for i, place in enumerate(places):
        start = pl.multiple_of(wanted[to[place]] * BLK, BLK)
        copies.append(
            pltpu.make_async_copy(candidates.at[pl.ds(start, BLK)], outs[i], sem.at[i])
        )
    for copy in copies:
        copy.start()
    for copy in copies:
        copy.wait()


def take_blocks(places, wanted, to, candidates):
    smem = pl.BlockSpec(memory_space=pltpu.SMEM)
    hbm = pl.BlockSpec(memory_space=pl.ANY)
    return list(
        pl.pallas_call(
            functools.partial(take_kernel, tuple(places)),
            out_shape=(
                jax.ShapeDtypeStruct((BLK, candidates.shape[1]), candidates.dtype),
            )
            * len(places),
            in_specs=[smem, smem, pl.BlockSpec(memory_space=pltpu.HBM)],
            out_specs=(hbm,) * len(places),
            scratch_shapes=[pltpu.SemaphoreType.DMA((len(places),))],
            compiler_params=pltpu.CompilerParams(vmem_limit_bytes=1 << 20),
            name="take_%d" % len(places),
        )(wanted, to, pltpu.with_memory_space_constraint(candidates, pltpu.HBM))
    )


def score_pairs(call, unroll, sources, zero_fill, n_pairs, meta, queries, inv_q, *out):
    n_src = len(sources)
    feature_dim = queries.shape[1]
    blocks = queries.shape[0] // BLK
    pairs_here = max(n_pairs * n_src // 16, 1)
    hbm = pl.BlockSpec(memory_space=pl.ANY)
    vmem = pl.BlockSpec(memory_space=pltpu.VMEM)
    return pl.pallas_call(
        functools.partial(pair_kernel, call, n_src, unroll, zero_fill, feature_dim),
        out_shape=(
            jax.ShapeDtypeStruct((n_pairs, BLK, BLK), jnp.bfloat16),
            jax.ShapeDtypeStruct((blocks, BLK), jnp.float32),
        ),
        in_specs=[pl.BlockSpec(memory_space=pltpu.SMEM), vmem, vmem]
        + [hbm] * (n_src + len(out)),
        out_specs=(hbm, vmem),
        scratch_shapes=[
            pltpu.VMEM((n_src, BLK, feature_dim), jnp.bfloat16),
            pltpu.VMEM((n_src, 1, BLK), jnp.float32),
            pltpu.VMEM((blocks, BLK, LANES), jnp.float32),
            pltpu.VMEM((2 * unroll, BLK, BLK), jnp.bfloat16),
            pltpu.VMEM((BLK, BLK), jnp.bfloat16),
            pltpu.SemaphoreType.DMA((n_src,)),
            pltpu.SemaphoreType.DMA((n_pairs,)),
        ],
        input_output_aliases={3 + n_src: 0} if out else {},
        cost_estimate=pl.CostEstimate(
            flops=2 * pairs_here * BLK * BLK * feature_dim,
            bytes_accessed=pairs_here * BLK * BLK * 2,
            transcendentals=0,
        ),
        compiler_params=pltpu.CompilerParams(vmem_limit_bytes=12 << 20),
        name="pairs_%d" % call,
    )(meta, queries, inv_q, *sources, *out)


def per_device(queries, candidates, requests, pairs, counts):
    row_count = lax.axis_size("rows")
    side = math.isqrt(row_count)
    col_count = lax.axis_size("cols")
    feature_dim = queries.shape[1]
    pair_count = pairs.shape[0]
    me = lax.axis_index("rows")
    my_y, my_z = me // side, me % side
    wanted = lax.all_to_all(requests, "rows", split_axis=0, concat_axis=0, tiled=True)[:, 0]

    odd = lax.axis_index("cols") % 2
    keys_of = []
    for parity in range(2):
        keys_of.append([0] * row_count)
        for call, (lo, hi, _, _) in enumerate(CALLS):
            for rank in range(lo, hi):
                dy, dz = PAIRED[rank - 1][parity] if rank else (0, 0)
                keys_of[parity][dy * side + dz] = (call * row_count + rank - lo) * 8
    slots = pairs[:, 1]
    away = ((my_y - slots // side) % side) * side + (my_z - slots % side) % side
    ids = jnp.arange(pair_count, dtype=jnp.int32)
    key = pairs[:, 0]
    for code, values in enumerate(zip(*keys_of)):
        key = key + jnp.where(away == code, jnp.where(odd == 1, values[1], values[0]), 0)
    key = jnp.where(ids < counts[0], key, CALL_LIMIT * row_count * 8)
    less = key[None, :] < key[:, None]
    twin = (key[None, :] == key[:, None]) & (ids[None, :] < ids[:, None])
    place = jnp.sum((less | twin).astype(jnp.int32), axis=1)
    lead = jnp.logical_not(jnp.any(twin, axis=1))
    tile = jnp.sum((less & lead[None, :]).astype(jnp.int32), axis=1)
    wide = jnp.arange(2 * pair_count, dtype=jnp.int32)
    at = place[None, :] == wide[:, None]
    sorted_ids = jnp.sum(jnp.where(at, ids[None, :], 0), axis=1)
    at = lead[None, :] & (tile[None, :] == wide[:, None])
    tile_key = jnp.sum(jnp.where(at, (key % (row_count * 8))[None, :], 0), axis=1)
    first_pair = jnp.sum(jnp.where(at, (place - pair_count)[None, :], 0), axis=1) + pair_count
    below = lead[None, :] & (key[None, :] < (wide * (row_count * 8))[:, None])
    starts = jnp.sum(below.astype(jnp.int32), axis=1)
    starts = jnp.where(wide == CALL_LIMIT, counts[0], starts)
    meta = jnp.stack([sorted_ids, tile_key, first_pair, starts])

    along = [
        [jnp.array([step[parity][axis] for step in PAIRED] + [0], jnp.int32) for axis in (0, 1)]
        for parity in (0, 1)
    ]
    dys, dzs = (jnp.where(odd == 1, along[1][axis], along[0][axis]) for axis in (0, 1))
    to = ((my_y + dys) % side) * side + (my_z + dzs) % side
    sends = take_blocks(range(HEAD), wanted, to, candidates)
    arrived = [None]
    out, sums, scored = None, [], 0

    def score(out, scored):
        lo, hi, unroll, _ = CALLS[scored]
        out, part = score_pairs(
            scored, unroll, arrived[lo:hi], scored == 0, pair_count, meta, queries, inv_q,
            *(() if out is None else (out,)),
        )
        sums.append(part)
        return out

    for k, step in enumerate(PAIRED):
        if k == HEAD:
            to = lax.optimization_barrier((to, arrived[1]))[0]
            sends += take_blocks(range(HEAD, row_count), wanted, to, candidates)
            arrived[0] = sends.pop()
            inv_q = inverse_norm(lax.optimization_barrier((queries, arrived[1]))[0])
            inv_q = jnp.broadcast_to(inv_q[:, None], (queries.shape[0], LANES))
        send = sends[k]
        if scored < len(CALLS) and CALLS[scored][3] == k:
            out = score(out, scored)
            scored += 1
        if sums:
            send = lax.optimization_barrier((send, sums[-1]))[0]
        perm = []
        for y in range(side):
            for z in range(side):
                for col in range(col_count):
                    dy, dz = step[col % 2]
                    target = ((y + dy) % side) * side + (z + dz) % side
                    perm.append(((y * side + z) * col_count + col, target * col_count + col))
        arrived.append(lax.ppermute(send, ("rows", "cols"), perm))
    while scored < len(CALLS):
        out = score(out, scored)
        scored += 1
    local = functools.reduce(jnp.add, sums)
    totals = local.reshape(-1)

    def other(values, flip):
        return lax.ppermute(values, "cols", [(i, i ^ flip) for i in range(col_count)])

    totals = totals + other(totals, 1)
    totals = (totals + other(totals, 2)) + (other(totals, 4) + other(totals, 6))
    return out, totals * (1.0 / BLK)


def solution(mesh):
    in_specs = (
        P("rows", None),
        P(("rows", "cols"), None),
        P(("rows", "cols"), None),
        P(("rows", "cols"), None),
        P(("rows", "cols")),
    )
    out_specs = (P(("rows", "cols"), None, None), P("rows"))
    return jax.shard_map(
        per_device, mesh=mesh, in_specs=in_specs, out_specs=out_specs, check_vma=False
    )
```
